128 devices in a mesh: row: 4 (over z_lo, core), col: 16 (over y, x), filt: 2 (over z_hi).
Axes of the slice: x: 4, y: 4, z: 4 (z_hi: 2, z_lo: 2; z = z_hi * 2 + z_lo), core: 2. Of those that a mesh axis runs over, the one named last changes fastest.
Arguments:
- grad_out: bfloat16 [16, 128, 256, 256], P(None, 'row', 'col', 'filt'), may hold values from -6 to 6
- pre_act: bfloat16 [16, 128, 256, 256], P(None, 'row', 'col', 'filt'), may hold values from -6 to 6
- weight_one: bfloat16 [3, 3, 256, 256], replicated, may hold values from -0.125 to 0.125
- weight_two: bfloat16 [3, 3, 256, 256], replicated, may hold values from -0.125 to 0.125
Outputs:
- grad_in: bfloat16 [16, 128, 256, 256], P(None, 'row', 'col', 'filt')
The draws below stay inside these ranges and needn't reach their ends.
All inputs are finite; a program needn't handle non-finite values.
Results may differ from the reference program's by a relative error of at most 0.0049.
Values may be sent and summed in bfloat16 or wider, within the bound.
No kernel may reach another device: no remote copies, remote signals or barrier semaphores. Data moves between devices by JAX's collectives and lax.ppermute only.
A program may use at most 192 MiB of HBM per device.

```python
import jax
import jax.numpy as jnp

C = 256
BATCH = 16
H = 128
W = 256


def block_scale(rng, extent, cuts, low, largest):
    def one(position, blocks):
        draws = jax.random.uniform(jax.random.fold_in(jax.random.fold_in(rng, 6), position), (blocks,), jnp.float32, low / len(cuts), largest / len(cuts))
        return jnp.repeat(jnp.exp(draws), extent[position] // blocks).reshape((-1,) + (1,) * (len(extent) - position - 1))

    level = one(*cuts[0])
    for cut in cuts[1:]:
        level = level * one(*cut)
    return level


def noise(key, shape, width, bound, split=(), kind=jnp.bfloat16):
    drawn = jax.random.normal(key, shape, jnp.float32) * width
    if len(split) > 0:
        drawn = block_scale(key, shape, split, -0.22, 0.18) * drawn
    return jnp.clip(drawn, min=-bound, max=bound).astype(kind)


def setup_inputs(seed: int = 0) -> dict:
    keys = jax.random.split(jax.random.key(seed), 5)
    grad_out = noise(keys[0], (BATCH, H, W, C), 1.0, 6.0, ((1, 4), (2, 16), (3, 2)))
    pre_act = noise(keys[1], (BATCH, H, W, C), 1.0, 6.0, ((1, 4), (2, 16), (3, 2)))
    weight_one = noise(keys[2], (3, 3, C, C), (9 * C) ** -0.5, 0.125)
    weight_two = noise(keys[3], (3, 3, C, C), (9 * C) ** -0.5, 0.125)
    return dict(grad_out=grad_out, pre_act=pre_act, weight_one=weight_one, weight_two=weight_two)


def back_conv(grad, weight, spacing):
    rows = grad.shape[1]
    cols = grad.shape[2]
    padded = jnp.pad(grad.astype(jnp.float32), ((0, 0), (spacing, spacing), (spacing, spacing), (0, 0)))
    total = jnp.zeros(grad.shape[:3] + (weight.shape[2],), jnp.float32)
    for tap_row in range(3):
        for tap_col in range(3):
            top = spacing * (2 - tap_row)
            left = spacing * (2 - tap_col)
            piece = padded[:, top:top + rows, left:left + cols, :]
            total = total + jnp.einsum("bhwo,io->bhwi", piece, weight[tap_row, tap_col].astype(jnp.float32))
    return total


def reference(grad_out, pre_act, weight_one, weight_two):
    grad_a = back_conv(grad_out, weight_two, 4)
    grad_h = jnp.where(pre_act > 0, grad_a, jnp.float32(0.0)).astype(jnp.bfloat16)
    return back_conv(grad_h, weight_one, 2).astype(jnp.bfloat16)
```

```python
import jax
import jax.numpy as jnp
from jax import lax
from jax.experimental import pallas as pl
from jax.experimental.pallas import tpu as pltpu
from jax.sharding import PartitionSpec as P

CHUNKS = (4, 4)
FAR = 4
NEAR = 2
SPREAD = FAR + NEAR


def from_before(x, axis):
    count = lax.axis_size(axis)
    return lax.ppermute(x, axis, [(i, i + 1) for i in range(count - 1)])


def from_after(x, axis):
    count = lax.axis_size(axis)
    return lax.ppermute(x, axis, [(i + 1, i) for i in range(count - 1)])


def to_partner(x):
    return lax.ppermute(x, "filt", [(0, 1), (1, 0)])


def relative_weight(weight, part):
    taps = weight.shape[:2]
    channels = weight.shape[2]
    half = channels // 2
    swapped = jnp.roll(weight, (half, half), (2, 3))
    own_first = jnp.where(part == 0, weight, swapped)
    turned = own_first[:, ::-1].transpose(0, 1, 3, 2)
    return turned.reshape(taps[0], taps[1] * channels, channels)


def fill_shifted(shifted, middle, left, right, spacing):
    rows, cols, channels = middle.shape
    shifted[:, spacing:, :channels] = middle[:, : cols - spacing]
    shifted[:, :spacing, :channels] = left
    shifted[:, :, channels : 2 * channels] = middle
    shifted[:, : cols - spacing, 2 * channels :] = middle[:, spacing:]
    shifted[:, cols - spacing :, 2 * channels :] = right


def taps_sum(shifted, weight_ref, spacing, rows):
    cols, depth = shifted.shape[1:]
    total = None
    for tap_row in range(3):
        top = spacing * (2 - tap_row)
        piece = shifted[top : top + rows].reshape(rows * cols, depth)
        term = jnp.dot(piece, weight_ref[tap_row], preferred_element_type=jnp.float32)
        total = term if total is None else total + term
    return total


def first_kernel(part_ref, own, other, top, bottom, left, right, gate_own, gate_other, weight, grad_h, edge_left, edge_right, whole, shifted):
    rows = own.shape[1]
    half = own.shape[3]
    whole[:SPREAD] = top[0]
    whole[SPREAD : SPREAD + rows, :, :half] = own[0]
    whole[SPREAD : SPREAD + rows, :, half:] = other[0]
    whole[SPREAD + rows :] = bottom[0]
    fill_shifted(shifted, whole[...], left[0], right[0], FAR)
    out_rows = rows + 2 * NEAR
    total = taps_sum(shifted, weight, FAR, out_rows).reshape(out_rows, own.shape[2], 2 * half)
    kept_own = jnp.where(gate_own[0].astype(jnp.float32) > 0, total[:, :, :half], 0.0).astype(jnp.bfloat16)
    kept_other = jnp.where(gate_other[0].astype(jnp.float32) > 0, total[:, :, half:], 0.0).astype(jnp.bfloat16)
    grad_h[0, :, :, :half] = kept_own
    grad_h[0, :, :, half:] = kept_other
    cols = own.shape[2]
    edge_left[0] = grad_h[0, :, :NEAR]
    edge_right[0] = grad_h[0, :, cols - NEAR :]


def second_kernel(grad_h, left, right, weight, kept, sent, shifted):
    fill_shifted(shifted, grad_h[0], left[0], right[0], NEAR)
    rows, cols, half = kept.shape[1:]
    total = taps_sum(shifted, weight, NEAR, rows).reshape(rows, cols, 2 * half).astype(jnp.bfloat16)
    kept[0] = total[:, :, :half]
    sent[0] = total[:, :, half:]


def per_device(grad_out, pre_act, weight_one, weight_two):
    batch, rows, cols, half = grad_out.shape
    mine = batch // 2
    part = lax.axis_index("filt")
    own_at = part * mine
    other_at = (1 - part) * mine
    channels = 2 * half

    other = to_partner(lax.dynamic_slice_in_dim(grad_out, other_at, mine, 0))
    own = lax.dynamic_slice_in_dim(grad_out, own_at, mine, 0)
    gate_top = from_before(pre_act[:, rows - NEAR :], "row")
    gate_bottom = from_after(pre_act[:, :NEAR], "row")
    gate = jnp.concatenate([gate_top, pre_act, gate_bottom], axis=1)
    gate_sent = lax.dynamic_slice_in_dim(gate, other_at, mine, 0)
    first_weight = relative_weight(weight_two, part)
    second_weight = relative_weight(weight_one, part)

    both = jnp.concatenate([own, other], axis=3)
    top = from_before(both[:, rows - SPREAD :], "row")
    bottom = from_after(both[:, :SPREAD], "row")
    tall = jnp.concatenate([top, both, bottom], axis=1)
    left = from_before(tall[:, :, cols - FAR :], "col")
    right = from_after(tall[:, :, :FAR], "col")

    tall_rows = rows + 2 * SPREAD
    gate_rows = rows + 2 * NEAR
    where = jnp.reshape(own_at, (1,)).astype(jnp.int32)
    result = jnp.zeros_like(grad_out)
    start = 0
    for size in CHUNKS:
        gate_other = to_partner(gate_sent[start : start + size])

        def by_own(i, ref, start=start):
            return (ref[0] + start + i, 0, 0, 0)

        def by_mine(i, ref, start=start):
            return (start + i, 0, 0, 0)

        def by_chunk(i, *refs):
            return (i, 0, 0, 0)

        def whole_weight(i, *refs):
            return (0, 0, 0)

        grad_h, edge_left, edge_right = pl.pallas_call(
            first_kernel,
            out_shape=(
                jax.ShapeDtypeStruct((size, gate_rows, cols, channels), jnp.bfloat16),
                jax.ShapeDtypeStruct((size, gate_rows, NEAR, channels), jnp.bfloat16),
                jax.ShapeDtypeStruct((size, gate_rows, NEAR, channels), jnp.bfloat16),
            ),
            grid_spec=pltpu.PrefetchScalarGridSpec(
                num_scalar_prefetch=1,
                grid=(size,),
                in_specs=[
                    pl.BlockSpec((1, rows, cols, half), by_own),
                    pl.BlockSpec((1, rows, cols, half), by_mine),
                    pl.BlockSpec((1, SPREAD, cols, channels), by_mine),
                    pl.BlockSpec((1, SPREAD, cols, channels), by_mine),
                    pl.BlockSpec((1, tall_rows, FAR, channels), by_mine),
                    pl.BlockSpec((1, tall_rows, FAR, channels), by_mine),
                    pl.BlockSpec((1, gate_rows, cols, half), by_own),
                    pl.BlockSpec((1, gate_rows, cols, half), by_chunk),
                    pl.BlockSpec((3, 3 * channels, channels), whole_weight),
                ],
                out_specs=(
                    pl.BlockSpec((1, gate_rows, cols, channels), by_chunk),
                    pl.BlockSpec((1, gate_rows, NEAR, channels), by_chunk),
                    pl.BlockSpec((1, gate_rows, NEAR, channels), by_chunk),
                ),
                scratch_shapes=[
                    pltpu.VMEM((tall_rows, cols, channels), jnp.bfloat16),
                    pltpu.VMEM((tall_rows, cols, 3 * channels), jnp.bfloat16),
                ],
            ),
            cost_estimate=pl.CostEstimate(flops=size * 2 * gate_rows * cols * 9 * channels * channels, bytes_accessed=size * 2**20, transcendentals=0),
            name="first",
        )(where, grad_out, other, top, bottom, left, right, gate, gate_other, first_weight)
        h_left = from_before(edge_right, "col")
        h_right = from_after(edge_left, "col")
        kept, sent = pl.pallas_call(
            second_kernel,
            out_shape=(
                jax.ShapeDtypeStruct((size, rows, cols, half), jnp.bfloat16),
                jax.ShapeDtypeStruct((size, rows, cols, half), jnp.bfloat16),
            ),
            grid=(size,),
            in_specs=[
                pl.BlockSpec((1, gate_rows, cols, channels), by_chunk),
                pl.BlockSpec((1, gate_rows, NEAR, channels), by_chunk),
                pl.BlockSpec((1, gate_rows, NEAR, channels), by_chunk),
                pl.BlockSpec((3, 3 * channels, channels), whole_weight),
            ],
            out_specs=(
                pl.BlockSpec((1, rows, cols, half), by_chunk),
                pl.BlockSpec((1, rows, cols, half), by_chunk),
            ),
            scratch_shapes=[pltpu.VMEM((gate_rows, cols, 3 * channels), jnp.bfloat16)],
            cost_estimate=pl.CostEstimate(flops=size * 2 * rows * cols * 9 * channels * channels, bytes_accessed=size * 2**20, transcendentals=0),
            name="second",
        )(grad_h, h_left, h_right, second_weight)
        back = to_partner(sent)
        result = lax.dynamic_update_slice_in_dim(result, kept, own_at + start, 0)
        result = lax.dynamic_update_slice_in_dim(result, back, other_at + start, 0)
        start += size
    return result


def solution(mesh):
    placed = (P(None, "row", "col", "filt"), P(None, "row", "col", "filt"), P(), P())
    return jax.shard_map(
        per_device,
        mesh=mesh,
        in_specs=placed,
        out_specs=P(None, "row", "col", "filt"),
        check_vma=False,
    )
```

```python
import jax
import jax.numpy as jnp
from jax import lax
from jax.experimental import pallas as pl
from jax.experimental.pallas import tpu as pltpu
from jax.sharding import PartitionSpec as P

CHUNKS = (4, 4)
FAR = 4
NEAR = 2
SPREAD = FAR + NEAR


def from_before(x, axis):
    count = lax.axis_size(axis)
    return lax.ppermute(x, axis, [(i, i + 1) for i in range(count - 1)])


def from_after(x, axis):
    count = lax.axis_size(axis)
    return lax.ppermute(x, axis, [(i + 1, i) for i in range(count - 1)])


def to_partner(x):
    return lax.ppermute(x, "filt", [(0, 1), (1, 0)])


def relative_weight(weight, part):
    taps = weight.shape[:2]
    channels = weight.shape[2]
    half = channels // 2
    swapped = jnp.roll(weight, (half, half), (2, 3))
    own_first = jnp.where(part == 0, weight, swapped)
    turned = own_first[:, ::-1].transpose(0, 1, 3, 2)
    return turned.reshape(taps[0], taps[1] * channels, channels)


def fill_shifted(shifted, middle, left, right, spacing):
    _, cols, channels = middle.shape
    shifted[:, spacing:, :channels] = middle[:, : cols - spacing]
    shifted[:, :spacing, :channels] = left
    shifted[:, :, channels : 2 * channels] = middle
    shifted[:, : cols - spacing, 2 * channels :] = middle[:, spacing:]
    shifted[:, cols - spacing :, 2 * channels :] = right


def taps_sum(shifted, weight_ref, spacing, rows):
    cols, depth = shifted.shape[1:]
    total = None
    for tap_row in range(3):
        top = spacing * (2 - tap_row)
        piece = shifted[top : top + rows].reshape(rows * cols, depth)
        term = jnp.dot(piece, weight_ref[tap_row], preferred_element_type=jnp.float32)
        total = term if total is None else total + term
    return total


def first_kernel(part_ref, own, other, top_own, top_other, bottom_own, bottom_other, left_own, left_other, right_own, right_other, gate_own, gate_other, weight, grad_h, edge_left, edge_right, whole, shifted):
    rows = own.shape[1]
    half = own.shape[3]
    halves = (
        (slice(0, half), own, top_own, bottom_own, left_own, right_own),
        (slice(half, 2 * half), other, top_other, bottom_other, left_other, right_other),
    )
    for lanes, middle, top, bottom, _, _ in halves:
        whole[:SPREAD, :, lanes] = top[0]
        whole[SPREAD : SPREAD + rows, :, lanes] = middle[0]
        whole[SPREAD + rows :, :, lanes] = bottom[0]
    left = jnp.concatenate([left_own[0], left_other[0]], axis=2)
    right = jnp.concatenate([right_own[0], right_other[0]], axis=2)
    fill_shifted(shifted, whole[...], left, right, FAR)
    out_rows = rows + 2 * NEAR
    total = taps_sum(shifted, weight, FAR, out_rows).reshape(out_rows, own.shape[2], 2 * half)
    kept_own = jnp.where(gate_own[0].astype(jnp.float32) > 0, total[:, :, :half], 0.0).astype(jnp.bfloat16)
    kept_other = jnp.where(gate_other[0].astype(jnp.float32) > 0, total[:, :, half:], 0.0).astype(jnp.bfloat16)
    grad_h[0, :, :, :half] = kept_own
    grad_h[0, :, :, half:] = kept_other
    cols = own.shape[2]
    edge_left[0] = grad_h[0, :, :NEAR]
    edge_right[0] = grad_h[0, :, cols - NEAR :]


def second_kernel(grad_h, left, right, weight, kept, sent, shifted):
    fill_shifted(shifted, grad_h[0], left[0], right[0], NEAR)
    rows, cols, half = kept.shape[1:]
    total = taps_sum(shifted, weight, NEAR, rows).reshape(rows, cols, 2 * half).astype(jnp.bfloat16)
    kept[0] = total[:, :, :half]
    sent[0] = total[:, :, half:]


def on_device(grad_out, pre_act, weight_one, weight_two):
    batch, rows, cols, half = grad_out.shape
    mine = batch // 2
    part = lax.axis_index("filt")
    own_at = part * mine
    other_at = (1 - part) * mine
    channels = 2 * half

    def halo_rows(x):
        return from_before(x[:, rows - SPREAD :], "row"), from_after(x[:, :SPREAD], "row")

    def halo_cols(x, top, bottom):
        last = [piece[:, :, cols - FAR :] for piece in (top, x, bottom)]
        first = [piece[:, :, :FAR] for piece in (top, x, bottom)]
        return from_before(jnp.concatenate(last, axis=1), "col"), from_after(jnp.concatenate(first, axis=1), "col")

    other = to_partner(lax.dynamic_slice_in_dim(grad_out, other_at, mine, 0))
    gate_top = from_before(pre_act[:, rows - NEAR :], "row")
    gate_bottom = from_after(pre_act[:, :NEAR], "row")
    gate = jnp.concatenate([gate_top, pre_act, gate_bottom], axis=1)
    own = lax.dynamic_slice_in_dim(grad_out, own_at, mine, 0)
    top_own, bottom_own = halo_rows(own)
    left_own, right_own = halo_cols(own, top_own, bottom_own)
    first_weight = relative_weight(weight_two, part)
    second_weight = relative_weight(weight_one, part)
    top_other, bottom_other = halo_rows(other)
    gate_others = []
    start = 0
    for size in CHUNKS:
        gate_others.append(to_partner(lax.dynamic_slice_in_dim(gate, other_at + start, size, 0)))
        start += size
    left_other, right_other = halo_cols(other, top_other, bottom_other)

    tall_rows = rows + 2 * SPREAD
    gate_rows = rows + 2 * NEAR
    where = jnp.reshape(own_at, (1,)).astype(jnp.int32)
    result = jnp.zeros_like(grad_out)
    start = 0
    for step, size in enumerate(CHUNKS):
        gate_other = gate_others[step]

        def by_own(i, ref, start=start):
            return (ref[0] + start + i, 0, 0, 0)

        def by_mine(i, ref, start=start):
            return (start + i, 0, 0, 0)

        def by_chunk(i, *refs):
            return (i, 0, 0, 0)

        def whole_weight(i, *refs):
            return (0, 0, 0)

        grad_h, edge_left, edge_right = pl.pallas_call(
            first_kernel,
            out_shape=(
                jax.ShapeDtypeStruct((size, gate_rows, cols, channels), jnp.bfloat16),
                jax.ShapeDtypeStruct((size, gate_rows, NEAR, channels), jnp.bfloat16),
                jax.ShapeDtypeStruct((size, gate_rows, NEAR, channels), jnp.bfloat16),
            ),
            grid_spec=pltpu.PrefetchScalarGridSpec(
                num_scalar_prefetch=1,
                grid=(size,),
                in_specs=[
                    pl.BlockSpec((1, rows, cols, half), by_own),
                    pl.BlockSpec((1, rows, cols, half), by_mine),
                    *[pl.BlockSpec((1, SPREAD, cols, half), by_mine)] * 4,
                    *[pl.BlockSpec((1, tall_rows, FAR, half), by_mine)] * 4,
                    pl.BlockSpec((1, gate_rows, cols, half), by_own),
                    pl.BlockSpec((1, gate_rows, cols, half), by_chunk),
                    pl.BlockSpec((3, 3 * channels, channels), whole_weight),
                ],
                out_specs=(
                    pl.BlockSpec((1, gate_rows, cols, channels), by_chunk),
                    pl.BlockSpec((1, gate_rows, NEAR, channels), by_chunk),
                    pl.BlockSpec((1, gate_rows, NEAR, channels), by_chunk),
                ),
                scratch_shapes=[
                    pltpu.VMEM((tall_rows, cols, channels), jnp.bfloat16),
                    pltpu.VMEM((tall_rows, cols, 3 * channels), jnp.bfloat16),
                ],
            ),
            cost_estimate=pl.CostEstimate(flops=size * 2 * gate_rows * cols * 9 * channels * channels, bytes_accessed=size * 2**20, transcendentals=0),
            name="first",
        )(where, grad_out, other, top_own, top_other, bottom_own, bottom_other, left_own, left_other, right_own, right_other, gate, gate_other, first_weight)
        h_left = from_before(edge_right, "col")
        h_right = from_after(edge_left, "col")
        kept, sent = pl.pallas_call(
            second_kernel,
            out_shape=(
                jax.ShapeDtypeStruct((size, rows, cols, half), jnp.bfloat16),
                jax.ShapeDtypeStruct((size, rows, cols, half), jnp.bfloat16),
            ),
            grid=(size,),
            in_specs=[
                pl.BlockSpec((1, gate_rows, cols, channels), by_chunk),
                pl.BlockSpec((1, gate_rows, NEAR, channels), by_chunk),
                pl.BlockSpec((1, gate_rows, NEAR, channels), by_chunk),
                pl.BlockSpec((3, 3 * channels, channels), whole_weight),
            ],
            out_specs=(
                pl.BlockSpec((1, rows, cols, half), by_chunk),
                pl.BlockSpec((1, rows, cols, half), by_chunk),
            ),
            scratch_shapes=[pltpu.VMEM((gate_rows, cols, 3 * channels), jnp.bfloat16)],
            cost_estimate=pl.CostEstimate(flops=size * 2 * rows * cols * 9 * channels * channels, bytes_accessed=size * 2**20, transcendentals=0),
            name="second",
        )(grad_h, h_left, h_right, second_weight)
        back = to_partner(sent)
        result = lax.dynamic_update_slice_in_dim(result, kept, own_at + start, 0)
        result = lax.dynamic_update_slice_in_dim(result, back, other_at + start, 0)
        start += size
    return result


def solution(mesh):
    placed = (P(None, "row", "col", "filt"), P(None, "row", "col", "filt"), P(), P())
    return jax.shard_map(
        on_device,
        mesh=mesh,
        in_specs=placed,
        out_specs=P(None, "row", "col", "filt"),
        check_vma=False,
    )
```

```python
import jax
import jax.numpy as jnp
from jax import lax
from jax.experimental import pallas as pl
from jax.experimental.pallas import tpu as pltpu
from jax.sharding import PartitionSpec as P

PARTS = (2, 3, 3)
FAR = 4
NEAR = 2
SPREAD = FAR + NEAR


def from_before(x, axis):
    count = lax.axis_size(axis)
    return lax.ppermute(x, axis, [(i, i + 1) for i in range(count - 1)])


def from_after(x, axis):
    count = lax.axis_size(axis)
    return lax.ppermute(x, axis, [(i + 1, i) for i in range(count - 1)])


def to_partner(x):
    return lax.ppermute(x, "filt", [(0, 1), (1, 0)])


def relative_weight(weight, part):
    taps = weight.shape[:2]
    channels = weight.shape[2]
    half = channels // 2
    swapped = jnp.roll(weight, (half, half), (2, 3))
    own_first = jnp.where(part == 0, weight, swapped)
    turned = own_first[:, ::-1].transpose(0, 1, 3, 2)
    return turned.reshape(taps[0], taps[1] * channels, channels)


def fill_shifted(shifted, middle, left, right, spacing):
    _, cols, channels = middle.shape
    shifted[:, spacing:, :channels] = middle[:, : cols - spacing]
    shifted[:, :spacing, :channels] = left
    shifted[:, :, channels : 2 * channels] = middle
    shifted[:, : cols - spacing, 2 * channels :] = middle[:, spacing:]
    shifted[:, cols - spacing :, 2 * channels :] = right


def taps_sum(shifted, weight_ref, spacing, rows):
    cols, depth = shifted.shape[1:]
    total = None
    for tap_row in range(3):
        top = spacing * (2 - tap_row)
        piece = shifted[top : top + rows].reshape(rows * cols, depth)
        term = jnp.dot(piece, weight_ref[tap_row], preferred_element_type=jnp.float32)
        total = term if total is None else total + term
    return total


def first_kernel(part_ref, own, other_a, other_b, top, bottom, left, right, gate_own, gate_other, weight, grad_h, edge_left, edge_right, whole, shifted):
    rows = own.shape[1]
    half = own.shape[3]
    early = pl.program_id(0) < pl.num_programs(0) // 2
    whole[:SPREAD] = top[0]
    whole[SPREAD : SPREAD + rows, :, :half] = own[0]

    @pl.when(early)
    def _():
        whole[SPREAD : SPREAD + rows, :, half:] = other_a[0]

    @pl.when(jnp.logical_not(early))
    def _():
        whole[SPREAD : SPREAD + rows, :, half:] = other_b[0]

    whole[SPREAD + rows :] = bottom[0]
    fill_shifted(shifted, whole[...], left[0], right[0], FAR)
    out_rows = rows + 2 * NEAR
    total = taps_sum(shifted, weight, FAR, out_rows).reshape(out_rows, own.shape[2], 2 * half)
    kept_own = jnp.where(gate_own[0].astype(jnp.float32) > 0, total[:, :, :half], 0.0).astype(jnp.bfloat16)
    kept_other = jnp.where(gate_other[0].astype(jnp.float32) > 0, total[:, :, half:], 0.0).astype(jnp.bfloat16)
    grad_h[0, :, :, :half] = kept_own
    grad_h[0, :, :, half:] = kept_other
    cols = own.shape[2]
    edge_left[0] = grad_h[0, :, :NEAR]
    edge_right[0] = grad_h[0, :, cols - NEAR :]


def second_kernel(grad_h, left, right, weight, kept, sent, shifted):
    fill_shifted(shifted, grad_h[0], left[0], right[0], NEAR)
    rows, cols, half = kept.shape[1:]
    total = taps_sum(shifted, weight, NEAR, rows).reshape(rows, cols, 2 * half).astype(jnp.bfloat16)
    kept[0] = total[:, :, :half]
    sent[0] = total[:, :, half:]


def on_device(grad_out, pre_act, weight_one, weight_two):
    batch, rows, cols, half = grad_out.shape
    mine = batch // 2
    part = lax.axis_index("filt")
    own_at = part * mine
    other_at = (1 - part) * mine
    channels = 2 * half

    few = mine // 2
    other_a = to_partner(lax.dynamic_slice_in_dim(grad_out, other_at, few, 0))
    gate_top = from_before(pre_act[:, rows - NEAR :], "row")
    gate_bottom = from_after(pre_act[:, :NEAR], "row")
    other_b = to_partner(lax.dynamic_slice_in_dim(grad_out, other_at + few, few, 0))
    gate = jnp.concatenate([gate_top, pre_act, gate_bottom], axis=1)
    own = lax.dynamic_slice_in_dim(grad_out, own_at, mine, 0)
    first_weight = relative_weight(weight_two, part)
    second_weight = relative_weight(weight_one, part)
    both = jnp.concatenate([own, jnp.concatenate([other_a, other_b], axis=0)], axis=3)
    top = from_before(both[:, rows - SPREAD :], "row")
    bottom = from_after(both[:, :SPREAD], "row")
    gate_other = to_partner(lax.dynamic_slice_in_dim(gate, other_at, mine, 0))
    last = [piece[:, :, cols - FAR :] for piece in (top, both, bottom)]
    left = from_before(jnp.concatenate(last, axis=1), "col")
    head = [piece[:, :, :FAR] for piece in (top, both, bottom)]
    right = from_after(jnp.concatenate(head, axis=1), "col")

    tall_rows = rows + 2 * SPREAD
    gate_rows = rows + 2 * NEAR
    where = jnp.reshape(own_at, (1,)).astype(jnp.int32)

    def by_own(i, ref):
        return (ref[0] + i, 0, 0, 0)

    def by_mine(i, *refs):
        return (i, 0, 0, 0)

    def whole_weight(i, *refs):
        return (0, 0, 0)

    grad_h, edge_left, edge_right = pl.pallas_call(
        first_kernel,
        out_shape=(
            jax.ShapeDtypeStruct((mine, gate_rows, cols, channels), jnp.bfloat16),
            jax.ShapeDtypeStruct((mine, gate_rows, NEAR, channels), jnp.bfloat16),
            jax.ShapeDtypeStruct((mine, gate_rows, NEAR, channels), jnp.bfloat16),
        ),
        grid_spec=pltpu.PrefetchScalarGridSpec(
            num_scalar_prefetch=1,
            grid=(mine,),
            in_specs=[
                pl.BlockSpec((1, rows, cols, half), by_own),
                pl.BlockSpec((1, rows, cols, half), lambda i, ref: (jnp.minimum(i, few - 1), 0, 0, 0)),
                pl.BlockSpec((1, rows, cols, half), lambda i, ref: (jnp.maximum(i - few, 0), 0, 0, 0)),
                pl.BlockSpec((1, SPREAD, cols, channels), by_mine),
                pl.BlockSpec((1, SPREAD, cols, channels), by_mine),
                pl.BlockSpec((1, tall_rows, FAR, channels), by_mine),
                pl.BlockSpec((1, tall_rows, FAR, channels), by_mine),
                pl.BlockSpec((1, gate_rows, cols, half), by_own),
                pl.BlockSpec((1, gate_rows, cols, half), by_mine),
                pl.BlockSpec((3, 3 * channels, channels), whole_weight),
            ],
            out_specs=(
                pl.BlockSpec((1, gate_rows, cols, channels), by_mine),
                pl.BlockSpec((1, gate_rows, NEAR, channels), by_mine),
                pl.BlockSpec((1, gate_rows, NEAR, channels), by_mine),
            ),
            scratch_shapes=[
                pltpu.VMEM((tall_rows, cols, channels), jnp.bfloat16),
                pltpu.VMEM((tall_rows, cols, 3 * channels), jnp.bfloat16),
            ],
        ),
        cost_estimate=pl.CostEstimate(flops=mine * 2 * gate_rows * cols * 9 * channels * channels, bytes_accessed=mine * 2**20, transcendentals=0),
        name="first",
    )(where, grad_out, other_a, other_b, top, bottom, left, right, gate, gate_other, first_weight)
    h_left = from_before(edge_right, "col")
    h_right = from_after(edge_left, "col")

    result = jnp.zeros_like(grad_out)
    start = 0
    for size in PARTS:

        def by_part(i, start=start):
            return (start + i, 0, 0, 0)

        def by_chunk(i):
            return (i, 0, 0, 0)

        kept, sent = pl.pallas_call(
            second_kernel,
            out_shape=(
                jax.ShapeDtypeStruct((size, rows, cols, half), jnp.bfloat16),
                jax.ShapeDtypeStruct((size, rows, cols, half), jnp.bfloat16),
            ),
            grid=(size,),
            in_specs=[
                pl.BlockSpec((1, gate_rows, cols, channels), by_part),
                pl.BlockSpec((1, gate_rows, NEAR, channels), by_part),
                pl.BlockSpec((1, gate_rows, NEAR, channels), by_part),
                pl.BlockSpec((3, 3 * channels, channels), whole_weight),
            ],
            out_specs=(
                pl.BlockSpec((1, rows, cols, half), by_chunk),
                pl.BlockSpec((1, rows, cols, half), by_chunk),
            ),
            scratch_shapes=[pltpu.VMEM((gate_rows, cols, 3 * channels), jnp.bfloat16)],
            cost_estimate=pl.CostEstimate(flops=size * 2 * rows * cols * 9 * channels * channels, bytes_accessed=size * 2**20, transcendentals=0),
            name="second",
        )(grad_h, h_left, h_right, second_weight)
        back = to_partner(sent)
        result = lax.dynamic_update_slice_in_dim(result, kept, own_at + start, 0)
        result = lax.dynamic_update_slice_in_dim(result, back, other_at + start, 0)
        start += size
    return result


def solution(mesh):
    placed = (P(None, "row", "col", "filt"), P(None, "row", "col", "filt"), P(), P())
    return jax.shard_map(
        on_device,
        mesh=mesh,
        in_specs=placed,
        out_specs=P(None, "row", "col", "filt"),
        check_vma=False,
    )
```

```python
import jax
import jax.numpy as jnp
from jax import lax
from jax.experimental import pallas as pl
from jax.experimental.pallas import tpu as pltpu
from jax.sharding import PartitionSpec as P

PARTS = (3, 5)
FAR = 4
NEAR = 2
SPREAD = FAR + NEAR


def from_before(x, axis):
    count = lax.axis_size(axis)
    return lax.ppermute(x, axis, [(i, i + 1) for i in range(count - 1)])


def from_after(x, axis):
    count = lax.axis_size(axis)
    return lax.ppermute(x, axis, [(i + 1, i) for i in range(count - 1)])


def to_partner(x):
    return lax.ppermute(x, "filt", [(0, 1), (1, 0)])


def relative_weight(weight, part):
    taps = weight.shape[:2]
    channels = weight.shape[2]
    half = channels // 2
    swapped = jnp.roll(weight, (half, half), (2, 3))
    own_first = jnp.where(part == 0, weight, swapped)
    turned = own_first[:, ::-1].transpose(0, 1, 3, 2)
    return turned.reshape(taps[0], taps[1] * channels, channels)


def fill_shifted(shifted, middle, left, right, spacing):
    _, cols, channels = middle.shape
    shifted[:, spacing:, :channels] = middle[:, : cols - spacing]
    shifted[:, :spacing, :channels] = left
    shifted[:, :, channels : 2 * channels] = middle
    shifted[:, : cols - spacing, 2 * channels :] = middle[:, spacing:]
    shifted[:, cols - spacing :, 2 * channels :] = right


def taps_sum(shifted, weight_ref, spacing, rows):
    cols, depth = shifted.shape[1:]
    total = None
    for tap_row in range(3):
        top = spacing * (2 - tap_row)
        piece = shifted[top : top + rows].reshape(rows * cols, depth)
        term = jnp.dot(piece, weight_ref[tap_row], preferred_element_type=jnp.float32)
        total = term if total is None else total + term
    return total


def first_kernel(part_ref, own, other_a, other_b, top, bottom, left, right, gate_own, gate_other, weight, grad_h, edge_left, edge_right, whole, shifted):
    rows = own.shape[1]
    half = own.shape[3]
    early = pl.program_id(0) < pl.num_programs(0) // 2
    whole[:SPREAD] = top[0]
    whole[SPREAD : SPREAD + rows, :, :half] = own[0]

    @pl.when(early)
    def _():
        whole[SPREAD : SPREAD + rows, :, half:] = other_a[0]

    @pl.when(jnp.logical_not(early))
    def _():
        whole[SPREAD : SPREAD + rows, :, half:] = other_b[0]

    whole[SPREAD + rows :] = bottom[0]
    fill_shifted(shifted, whole[...], left[0], right[0], FAR)
    out_rows = rows + 2 * NEAR
    total = taps_sum(shifted, weight, FAR, out_rows).reshape(out_rows, own.shape[2], 2 * half)
    kept_own = jnp.where(gate_own[0].astype(jnp.float32) > 0, total[:, :, :half], 0.0).astype(jnp.bfloat16)
    kept_other = jnp.where(gate_other[0].astype(jnp.float32) > 0, total[:, :, half:], 0.0).astype(jnp.bfloat16)
    grad_h[0, :, :, :half] = kept_own
    grad_h[0, :, :, half:] = kept_other
    cols = own.shape[2]
    edge_left[0] = grad_h[0, :, :NEAR]
    edge_right[0] = grad_h[0, :, cols - NEAR :]


def second_kernel(grad_h, left, right, weight, kept, sent, shifted):
    fill_shifted(shifted, grad_h[0], left[0], right[0], NEAR)
    rows, cols, half = kept.shape[1:]
    total = taps_sum(shifted, weight, NEAR, rows).reshape(rows, cols, 2 * half).astype(jnp.bfloat16)
    kept[0] = total[:, :, :half]
    sent[0] = total[:, :, half:]


def on_device(grad_out, pre_act, weight_one, weight_two):
    batch, rows, cols, half = grad_out.shape
    mine = batch // 2
    part = lax.axis_index("filt")
    own_at = part * mine
    other_at = (1 - part) * mine
    channels = 2 * half

    few = mine // 2
    other_a = to_partner(lax.dynamic_slice_in_dim(grad_out, other_at, few, 0))
    late, gate_last = lax.optimization_barrier((grad_out, pre_act[:, rows - NEAR :]))
    gate_top = from_before(gate_last, "row")
    gate_bottom = from_after(pre_act[:, :NEAR], "row")
    other_b = to_partner(lax.dynamic_slice_in_dim(late, other_at + few, few, 0))
    gate = jnp.concatenate([gate_top, pre_act, gate_bottom], axis=1)
    own = lax.dynamic_slice_in_dim(grad_out, own_at, mine, 0)
    first_weight = relative_weight(weight_two, part)
    second_weight = relative_weight(weight_one, part)
    both = jnp.concatenate([own, jnp.concatenate([other_a, other_b], axis=0)], axis=3)
    top = from_before(both[:, rows - SPREAD :], "row")
    bottom = from_after(both[:, :SPREAD], "row")
    gate_other = to_partner(lax.dynamic_slice_in_dim(gate, other_at, mine, 0))
    tall = jnp.concatenate([top, both, bottom], axis=1)
    left = from_before(tall[:, :, cols - FAR :], "col")
    right = from_after(tall[:, :, :FAR], "col")

    tall_rows = rows + 2 * SPREAD
    gate_rows = rows + 2 * NEAR
    where = jnp.reshape(own_at, (1,)).astype(jnp.int32)

    def by_own(i, ref):
        return (ref[0] + i, 0, 0, 0)

    def by_mine(i, *refs):
        return (i, 0, 0, 0)

    def whole_weight(i, *refs):
        return (0, 0, 0)

    grad_h, edge_left, edge_right = pl.pallas_call(
        first_kernel,
        out_shape=(
            jax.ShapeDtypeStruct((mine, gate_rows, cols, channels), jnp.bfloat16),
            jax.ShapeDtypeStruct((mine, gate_rows, NEAR, channels), jnp.bfloat16),
            jax.ShapeDtypeStruct((mine, gate_rows, NEAR, channels), jnp.bfloat16),
        ),
        grid_spec=pltpu.PrefetchScalarGridSpec(
            num_scalar_prefetch=1,
            grid=(mine,),
            in_specs=[
                pl.BlockSpec((1, rows, cols, half), by_own),
                pl.BlockSpec((1, rows, cols, half), lambda i, ref: (jnp.minimum(i, few - 1), 0, 0, 0)),
                pl.BlockSpec((1, rows, cols, half), lambda i, ref: (jnp.maximum(i - few, 0), 0, 0, 0)),
                pl.BlockSpec((1, SPREAD, cols, channels), by_mine),
                pl.BlockSpec((1, SPREAD, cols, channels), by_mine),
                pl.BlockSpec((1, tall_rows, FAR, channels), by_mine),
                pl.BlockSpec((1, tall_rows, FAR, channels), by_mine),
                pl.BlockSpec((1, gate_rows, cols, half), by_own),
                pl.BlockSpec((1, gate_rows, cols, half), by_mine),
                pl.BlockSpec((3, 3 * channels, channels), whole_weight),
            ],
            out_specs=(
                pl.BlockSpec((1, gate_rows, cols, channels), by_mine),
                pl.BlockSpec((1, gate_rows, NEAR, channels), by_mine),
                pl.BlockSpec((1, gate_rows, NEAR, channels), by_mine),
            ),
            scratch_shapes=[
                pltpu.VMEM((tall_rows, cols, channels), jnp.bfloat16),
                pltpu.VMEM((tall_rows, cols, 3 * channels), jnp.bfloat16),
            ],
        ),
        cost_estimate=pl.CostEstimate(flops=mine * 2 * gate_rows * cols * 9 * channels * channels, bytes_accessed=mine * 2**20, transcendentals=0),
        name="first",
    )(where, grad_out, other_a, other_b, top, bottom, left, right, gate, gate_other, first_weight)
    h_left = from_before(edge_right, "col")
    h_right = from_after(edge_left, "col")

    result = jnp.zeros_like(grad_out)
    start = 0
    for size in PARTS:

        def by_part(i, start=start):
            return (start + i, 0, 0, 0)

        def by_chunk(i):
            return (i, 0, 0, 0)

        kept, sent = pl.pallas_call(
            second_kernel,
            out_shape=(
                jax.ShapeDtypeStruct((size, rows, cols, half), jnp.bfloat16),
                jax.ShapeDtypeStruct((size, rows, cols, half), jnp.bfloat16),
            ),
            grid=(size,),
            in_specs=[
                pl.BlockSpec((1, gate_rows, cols, channels), by_part),
                pl.BlockSpec((1, gate_rows, NEAR, channels), by_part),
                pl.BlockSpec((1, gate_rows, NEAR, channels), by_part),
                pl.BlockSpec((3, 3 * channels, channels), whole_weight),
            ],
            out_specs=(
                pl.BlockSpec((1, rows, cols, half), by_chunk),
                pl.BlockSpec((1, rows, cols, half), by_chunk),
            ),
            scratch_shapes=[pltpu.VMEM((gate_rows, cols, 3 * channels), jnp.bfloat16)],
            cost_estimate=pl.CostEstimate(flops=size * 2 * rows * cols * 9 * channels * channels, bytes_accessed=size * 2**20, transcendentals=0),
            name="second",
        )(grad_h, h_left, h_right, second_weight)
        back = to_partner(sent)
        result = lax.dynamic_update_slice_in_dim(result, kept, own_at + start, 0)
        result = lax.dynamic_update_slice_in_dim(result, back, other_at + start, 0)
        start += size
    return result


def solution(mesh):
    placed = (P(None, "row", "col", "filt"), P(None, "row", "col", "filt"), P(), P())
    return jax.shard_map(
        on_device,
        mesh=mesh,
        in_specs=placed,
        out_specs=P(None, "row", "col", "filt"),
        check_vma=False,
    )
```
